32 devices in a mesh: pair: 16 (over z, y, core), split: 2 (over x).
Axes of the slice: x: 2, y: 2, z: 4, core: 2. Of those that a mesh axis runs over, the one named last changes fastest.
Arguments:
- descriptors: bfloat16 [16, 1024, 256], P('pair', 'split'), as said below
- points: bfloat16 [16, 3, 1024], P('pair', None, 'split'), may hold values from -6 to 6
- normals: bfloat16 [16, 3, 1024], P('pair', None, 'split'), may hold values from -6 to 6
- pair_list: int32 [384, 2], replicated, may hold values from 0 to 15, as said below
- intersection: int32 [384], P('pair'), may hold values from 256 to 1024
- pose_index: int32 [16], replicated, may hold values from 0 to 15, each once
Outputs:
- pair_cross: float32 [384, 6, 6], P('pair')
- pose_hessian: float32 [16, 6, 6], P('pair')
- pose_gradient: float32 [16, 6], P('pair')
The draws below stay inside these ranges and needn't reach their ends.
Inputs may be any that keep to these rules, and one draw needn't show every extreme that they name: `descriptors`: values stay within -24 to 24. `pair_list`: task k's source scan is scan k // 24. The owner of a scan s is s; a task's target has another owner than its source. Among the 24 tasks of one aligned block (tasks k // 24 alike), no owner holds the targets of more than 2 of them, and some owner holds exactly 2.
All inputs are finite; a program needn't handle non-finite values.
Results may differ from the reference program's by a relative error of at most 0.0003.
Values may be sent and summed in bfloat16 or wider, within the bound.
A program may use at most 64 MiB of HBM per device.

```python
import jax
import jax.numpy as jnp
from jax import lax

C = 256
S = 1024
SCAN_DEV = 1
PAIR_DEV = 24
CAP = 2
SCANS = 16
PAIRS = 384
N_PAIR = 16


def draw_descriptors(key, part):
    key_base = jax.random.fold_in(key, 0)
    values = jnp.clip(jax.random.normal(key_base, (SCANS, S, C), jnp.float32), -4.0, 4.0)
    return values.astype(jnp.bfloat16)


def draw_pair_list(key, part):
    key_source, key_order, key_local = jax.random.split(key, 3)
    owners = jnp.arange(N_PAIR, dtype=jnp.int32)
    source_local = jax.random.randint(key_source, (N_PAIR, PAIR_DEV), 0, SCAN_DEV, jnp.int32)
    sources = owners[:, None] * SCAN_DEV + source_local
    order_keys = jax.random.split(key_order, N_PAIR * CAP)
    offsets = jax.vmap(lambda single: jax.random.permutation(single, N_PAIR - 1))(order_keys)
    offsets = offsets.reshape(N_PAIR, CAP * (N_PAIR - 1))[:, :PAIR_DEV].astype(jnp.int32)
    holder = (owners[:, None] + 1 + offsets) % N_PAIR
    targets = holder * SCAN_DEV + jax.random.randint(key_local, (N_PAIR, PAIR_DEV), 0, SCAN_DEV, jnp.int32)
    return jnp.stack([sources, targets], axis=-1).reshape(PAIRS, 2).astype(jnp.int32)


def with_ends(values, key, least, largest):
    index_at = [jax.random.randint(jax.random.fold_in(key, axis), (), 0, length) for axis, length in enumerate(values.shape)]
    widest = values.shape.index(max(values.shape))
    neighbour = index_at[:widest] + [(index_at[widest] + 1) % values.shape[widest]] + index_at[widest + 1:]
    return values.at[tuple(index_at)].set(least).at[tuple(neighbour)].set(largest)


def block_levels(own_key, extent, pieces, least, top_value):
    def one(position, shards_of):
        draws = jax.random.uniform(jax.random.fold_in(jax.random.fold_in(own_key, 6), position), (shards_of,), jnp.float32, least / len(pieces), top_value / len(pieces))
        return jnp.repeat(jnp.exp(draws), extent[position] // shards_of).reshape((-1,) + (1,) * (len(extent) - position - 1))

    gain = one(*pieces[0])
    for cut in pieces[1:]:
        gain = gain * one(*cut)
    return gain


def noise(key, shape, spread, most, shards=(), kind=jnp.bfloat16):
    values = jax.random.normal(key, shape, jnp.float32) * spread
    if len(shards) > 0:
        values = block_levels(key, shape, shards, -0.22, 0.18) * values
    return jnp.clip(values, min=-most, max=most).astype(kind)


def setup_inputs(seed: int = 0) -> dict:
    key_list = jax.random.split(jax.random.key(seed), 7)
    return {
        "descriptors": draw_descriptors(jax.random.fold_in(key_list[6], 71), 0),
        "points": noise(key_list[1], (SCANS, 3, S), 1.0, 6.0, ((0, 16), (2, 2))),
        "normals": noise(key_list[2], (SCANS, 3, S), 1.0, 6.0, ((0, 16), (2, 2))),
        "pair_list": draw_pair_list(jax.random.fold_in(key_list[6], 71), 0),
        "intersection": with_ends(jax.random.randint(key_list[4], (PAIRS,), S // 4, S + 1), jax.random.fold_in(key_list[4], 1), S // 4, S).astype(jnp.int32),
        "pose_index": jax.random.permutation(key_list[5], SCANS).astype(jnp.int32),
    }


def cross_first(left_vec, right_vec):
    return jnp.stack([left_vec[1] * right_vec[2] - left_vec[2] * right_vec[1],
                      left_vec[2] * right_vec[0] - left_vec[0] * right_vec[2],
                      left_vec[0] * right_vec[1] - left_vec[1] * right_vec[0]], axis=0)


def reference(descriptors, points, normals, pair_list, intersection, pose_index):
    score_scale = descriptors.shape[2] ** -0.5
    row_ids = jnp.arange(S, dtype=jnp.int32)
    highest = lax.Precision.HIGHEST
    points_value = points.astype(jnp.float32)
    normals_value = normals.astype(jnp.float32)

    def one_task(task_row):
        source_id = task_row[0]
        target_id = task_row[1]
        live_rows = task_row[2]
        scores = jnp.dot(descriptors[source_id], descriptors[target_id].T, preferred_element_type=jnp.float32) * score_scale
        weights = jax.nn.softmax(scores, axis=1)
        geometry = jnp.concatenate([points_value[target_id], normals_value[target_id]], axis=0)
        softened = jnp.dot(geometry, weights.T, precision=highest)
        matched = softened[:3]
        normal = softened[3:]
        source = points_value[source_id]
        jacobian = jnp.concatenate([cross_first(source, normal), normal, -cross_first(matched, normal), -normal], axis=0)
        residual = jnp.sum(normal * (source - matched), axis=0)
        weight = (row_ids < live_rows).astype(jnp.float32)
        hessian = jnp.dot(jacobian * weight, jacobian.T, precision=highest) / S
        gradient = jnp.dot(jacobian * weight, residual, precision=highest) / S
        return hessian, gradient

    task_table = jnp.concatenate([pair_list, intersection[:, None]], axis=1).astype(jnp.int32)
    hessian, gradient = lax.map(one_task, task_table)
    pair_cross = hessian[:, :6, 6:]
    source_pose = pose_index[pair_list[:, 0]]
    target_pose = pose_index[pair_list[:, 1]]
    source_part = jnp.concatenate([hessian[:, :6, :6].reshape(-1, 36), gradient[:, :6]], axis=1)
    target_part = jnp.concatenate([hessian[:, 6:, 6:].reshape(-1, 36), gradient[:, 6:]], axis=1)
    pose_slots = jnp.arange(SCANS, dtype=jnp.int32)[:, None]
    onehot_source = (pose_slots == source_pose[None, :]).astype(jnp.float32)
    onehot_target = (pose_slots == target_pose[None, :]).astype(jnp.float32)
    totals = (jnp.dot(onehot_source, source_part, precision=highest) + jnp.dot(onehot_target, target_part, precision=highest)) / PAIR_DEV
    return pair_cross, totals[:, :36].reshape(-1, 6, 6), totals[:, 36:]
```

```python
import functools
import math

import jax
import jax.numpy as jnp
from jax import lax
from jax.experimental import pallas as pl
from jax.experimental.pallas import tpu as pltpu
from jax.sharding import PartitionSpec as P

NT = (((1,), (1,)), ((), ()))
NN = (((1,), (0,)), ((), ()))
PAD = 16


def fused(dims, meta, own_ref, pc_ref, ph_ref, pg_ref, blocks, src, mine, theirs, feats, tgrams, vown, vrecv,
          ring_send, ring_recv, part_send, part_recv, src_send, src_recv, par_send, par_recv, pose_send, pose_recv):
    n_pair, n_split, hr, width, tasks = dims
    half_ring = n_pair // 2
    reach = half_ring // 2
    n_sub = 2 * n_split
    rows = n_sub * hr
    factor = math.log2(math.e) * width ** -0.5
    p = lax.axis_index("pair")
    sp = lax.axis_index("split")
    core = p % 2
    group = p // 2
    partner = p + 1 - 2 * core
    odd = group % 2
    spot = (1 - odd) * (group // 2) + odd * (half_ring - 1 - group // 2)

    def pair_at(where, which):
        where = (where + half_ring) % half_ring
        late = where // reach
        return ((1 - late) * 2 * where + late * (2 * (half_ring - 1 - where) + 1)) * 2 + which

    def remote(a, b, s, r, device):
        return pltpu.make_async_remote_copy(a, b, s, r, device_id=device, device_id_type=pl.DeviceIdType.MESH)

    barrier = pltpu.get_barrier_semaphore()
    for f in range(1, n_pair):
        pl.semaphore_signal(barrier, inc=1, device_id={"pair": (p + f) % n_pair}, device_id_type=pl.DeviceIdType.MESH)
    for f in range(1, n_split):
        pl.semaphore_signal(barrier, inc=1, device_id={"split": (sp + f) % n_split}, device_id_type=pl.DeviceIdType.MESH)
    pl.semaphore_wait(barrier, n_pair + n_split - 2)

    goal = [pair_at(spot + 1, core), pair_at(spot - 1, core)]
    started = []

    def slot_of(way, d, which):
        return pair_at(spot - d if way == 0 else spot + d, which)

    def ring_copy(way, d, h, source):
        slot = slot_of(way, d, core)
        a = own_ref.at[h] if source else blocks.at[slot, h]
        return remote(a, blocks.at[slot, h], ring_send.at[way, d, h], ring_recv.at[way, d, h], {"pair": goal[way]})

    def ring_arrival(way, d, h):
        slot = slot_of(way, d, core)
        return remote(blocks.at[slot, h], blocks.at[slot, h], ring_send.at[way, d - 1, h], ring_recv.at[way, d - 1, h],
                      {"pair": goal[way]})

    def part_copy(way, d, h, source=False):
        slot = slot_of(way, d, core)
        a = own_ref.at[h] if source else blocks.at[slot, h]
        return remote(a, blocks.at[slot, h], part_send.at[way, d, h], part_recv.at[way, d, h], {"pair": partner})

    def part_arrival(way, d, h):
        slot = slot_of(way, d, 1 - core)
        return remote(blocks.at[slot, h], blocks.at[slot, h], part_send.at[way, d, h], part_recv.at[way, d, h],
                      {"pair": partner})

    def go(copy):
        copy.start()
        started.append(copy)

    for f in range(1, n_split):
        go(remote(own_ref, src.at[sp], src_send.at[f - 1], src_recv.at[f - 1], {"split": (sp + f) % n_split}))
    for h in range(2):
        for way in range(2):
            go(ring_copy(way, 0, h, True))
        go(part_copy(0, 0, h, True))
    src[sp] = own_ref[...]
    feats[p] = jnp.zeros_like(feats[p])
    for f in range(1, n_split):
        frm = (sp + n_split - f) % n_split
        remote(own_ref, src.at[frm], src_send.at[f - 1], src_recv.at[f - 1], {"split": frm}).wait_recv()

    row8 = lax.broadcasted_iota(jnp.int32, (8, hr), 0)

    def attend(slot):
        for u in range(n_sub):
            queries = src[u // 2, u % 2, :hr, :]
            scores = [lax.dot_general(blocks[slot, h, :hr, :], queries, NT, preferred_element_type=jnp.float32)
                      for h in range(2)]
            top = jnp.maximum(jnp.max(scores[0], axis=0, keepdims=True), jnp.max(scores[1], axis=0, keepdims=True))
            moment = None
            for h in range(2):
                weight = jnp.exp2((scores[h] - top) * factor)
                coarse = weight.astype(jnp.bfloat16)
                fine = (weight - coarse.astype(jnp.float32)).astype(jnp.bfloat16)
                shape = blocks[slot, h, hr:hr + PAD, :hr]
                for piece in (coarse, fine):
                    term = lax.dot_general(shape, piece, NN, preferred_element_type=jnp.float32)
                    moment = term if moment is None else moment + term
            mine[slot, u] = jnp.where(row8 == 7, top, moment[:8])

    order = []

    def process(items):
        slots = [slot_of(*item) for item in items]
        if len(slots) == 1:
            attend(slots[0])
        else:
            def body(k, carry):
                attend((1 - k) * slots[0] + k * slots[1])
                return carry
            lax.fori_loop(0, 2, body, 0)
        for slot in slots:
            index = len(order)
            order.append(slot)
            for f in range(1, n_split):
                go(remote(mine.at[slot], theirs.at[f - 1, slot], par_send.at[index, f - 1], par_recv.at[index, f - 1],
                          {"split": (sp + f) % n_split}))

    def take_partner(d, ways=(0, 1), halves=(0, 1)):
        for way in ways:
            for h in halves:
                part_arrival(way, d, h).wait_recv()

    for d in range(1, reach):
        for h in range(2):
            for way in range(2):
                ring_arrival(way, d, h).wait_recv()
                if d + 1 < reach or way == h:
                    go(ring_copy(way, d, h, False))
                go(part_copy(way, d, h))
            if h == 1:
                process([(0, d, core), (1, d, core)])
            elif d == 1:
                take_partner(0, (0,))
                process([(0, 0, 1 - core)])
            else:
                take_partner(d - 1)
                process([(0, d - 1, 1 - core), (1, d - 1, 1 - core)])
    take_partner(reach - 1)
    process([(0, reach - 1, 1 - core), (1, reach - 1, 1 - core)])
    for way in range(2):
        ring_arrival(way, reach, way).wait_recv()
        go(part_copy(way, reach, way))
    process([(0, reach, core)])
    for way in range(2):
        part_arrival(way, reach, way).wait_recv()
    process([(0, reach, 1 - core)])

    for index, slot in enumerate(order):
        for f in range(1, n_split):
            remote(mine.at[slot], theirs.at[f - 1, slot], par_send.at[index, f - 1], par_recv.at[index, f - 1],
                   {"split": (sp + f) % n_split}).wait_recv()

    def featurize(k, carry):
        slot = (p + 1 + k) % n_pair
        for u in range(n_sub):
            parts = [mine[slot, u]] + [theirs[f, slot, u] for f in range(n_split - 1)]
            top = parts[0][7:8]
            for part in parts[1:]:
                top = jnp.maximum(top, part[7:8])
            total = None
            for part in parts:
                term = part * jnp.exp2((part[7:8] - top) * factor)
                total = term if total is None else total + term
            soft = total / total[6:7]
            y = src[u // 2, u % 2, hr:hr + PAD, :hr].astype(jnp.float32)
            yv = [y[c:c + 1] for c in range(3)]
            mv = [soft[c:c + 1] for c in range(3)]
            nv = [soft[c:c + 1] for c in range(3, 6)]

            def cross(a, b):
                return [a[1] * b[2] - a[2] * b[1], a[2] * b[0] - a[0] * b[2], a[0] * b[1] - a[1] * b[0]]

            residual = nv[0] * (yv[0] - mv[0]) + nv[1] * (yv[1] - mv[1]) + nv[2] * (yv[2] - mv[2])
            zero = jnp.zeros_like(residual)
            minus = [-v for v in cross(mv, nv)] + [-v for v in nv]
            f16 = jnp.concatenate(cross(yv, nv) + nv + [residual, zero] + minus + [residual, zero], axis=0)
            coarse = f16.astype(jnp.bfloat16)
            fine = (f16 - coarse.astype(jnp.float32)).astype(jnp.bfloat16)
            feats[slot, :, u * hr:(u + 1) * hr] = jnp.concatenate([coarse, fine], axis=0)
        return carry

    lax.fori_loop(0, n_pair - 1, featurize, 0)

    lanes = 8 * n_pair
    row_ids = lax.broadcasted_iota(jnp.int32, (32, rows), 1)
    source_sum = jnp.zeros((8, 16), jnp.float32)
    for k in range(tasks):
        f = feats[meta[k]]
        live = jnp.where(row_ids < meta[tasks + k], f, jnp.zeros_like(f))
        gram = lax.dot_general(live, f, NT, preferred_element_type=jnp.float32)
        gram = gram[:16] + gram[16:]
        gram = (gram[:, :16] + gram[:, 16:]) * (1.0 / rows)
        pc_ref[k] = gram[0:6, 8:14]
        source_sum = source_sum + gram[:8]
        tgrams[k * 8:(k + 1) * 8, :] = gram[8:]
    spread_row = lax.broadcasted_iota(jnp.int32, (16, lanes), 0)
    spread_lane = lax.broadcasted_iota(jnp.int32, (16, lanes), 1)
    highest = lax.Precision.HIGHEST
    spread_target = (spread_lane % 8 == spread_row - 8).astype(jnp.float32)
    spread_source = (spread_lane % 8 == spread_row).astype(jnp.float32)
    wide = lax.dot_general(tgrams[...], spread_target, NN, precision=highest, preferred_element_type=jnp.float32)
    lane_scan = lax.broadcasted_iota(jnp.int32, (8, lanes), 1) // 8
    total = jnp.where(
        lane_scan == p,
        lax.dot_general(source_sum, spread_source, NN, precision=highest, preferred_element_type=jnp.float32), 0.0)
    for k in range(tasks):
        total = total + jnp.where(lane_scan == meta[k], wide[k * 8:(k + 1) * 8], 0.0)
    vown[...] = total
    for f in range(1, n_pair):
        go(remote(vown, vrecv.at[f - 1], pose_send.at[f - 1], pose_recv.at[f - 1], {"pair": (p + f) % n_pair}))
    scan = 0
    for k in range(n_pair):
        scan = scan + k * (meta[2 * tasks + k] == p).astype(jnp.int32)
    for f in range(1, n_pair):
        remote(vown, vrecv.at[f - 1], pose_send.at[f - 1], pose_recv.at[f - 1], {"pair": (p + f) % n_pair}).wait_recv()
    for f in range(n_pair - 1):
        total = total + vrecv[f]
    total = jnp.where(lane_scan == scan, total, 0.0) * (1.0 / tasks)
    gather_row = lax.broadcasted_iota(jnp.int32, (8, lanes), 0)
    gather_lane = lax.broadcasted_iota(jnp.int32, (8, lanes), 1)
    pick = (gather_lane % 8 == gather_row).astype(jnp.float32)
    result = lax.dot_general(total, pick, NT, precision=highest, preferred_element_type=jnp.float32)
    ph_ref[0] = result[0:6, 0:6]
    pg_ref[...] = result[6:7, 0:6]
    for copy in started:
        copy.wait_send()


def per_device(n_pair, n_split, descriptors, points, normals, pair_list, intersection, pose_index):
    block_rows, width = descriptors.shape[1:]
    hr = block_rows // 2
    tasks = intersection.shape[0]
    p = lax.axis_index("pair")
    targets = lax.dynamic_slice_in_dim(pair_list[:, 1], p * tasks, tasks, 0)
    meta = jnp.concatenate([targets, intersection, pose_index])
    geometry = jnp.concatenate(
        [points[0], normals[0], jnp.ones((1, block_rows), points.dtype), jnp.zeros((PAD - 7, block_rows), points.dtype)], axis=0)
    geometry = geometry.reshape(PAD, 2, hr).transpose(1, 0, 2)
    geometry = jnp.pad(geometry, ((0, 0), (0, 0), (0, width - hr)))
    own = jnp.concatenate([descriptors[0].reshape(2, hr, width), geometry], axis=1)
    n_sub = 2 * n_split
    reach = n_pair // 4
    peers = max(n_split - 1, 1)
    dims = (n_pair, n_split, hr, width, tasks)
    dma = pltpu.SemaphoreType.DMA
    vmem = pl.BlockSpec(memory_space=pltpu.VMEM)
    return pl.pallas_call(
        functools.partial(fused, dims),
        out_shape=(
            jax.ShapeDtypeStruct((tasks, 6, 6), jnp.float32),
            jax.ShapeDtypeStruct((1, 6, 6), jnp.float32),
            jax.ShapeDtypeStruct((1, 6), jnp.float32),
        ),
        in_specs=[pl.BlockSpec(memory_space=pltpu.SMEM), vmem],
        out_specs=(vmem, vmem, vmem),
        scratch_shapes=[
            pltpu.VMEM((n_pair, 2, hr + PAD, width), jnp.bfloat16),
            pltpu.VMEM((n_split, 2, hr + PAD, width), jnp.bfloat16),
            pltpu.VMEM((n_pair, n_sub, 8, hr), jnp.float32),
            pltpu.VMEM((peers, n_pair, n_sub, 8, hr), jnp.float32),
            pltpu.VMEM((n_pair, 32, n_sub * hr), jnp.bfloat16),
            pltpu.VMEM((tasks * 8, 16), jnp.float32),
            pltpu.VMEM((8, 8 * n_pair), jnp.float32),
            pltpu.VMEM((n_pair - 1, 8, 8 * n_pair), jnp.float32),
            dma((2, reach, 2)), dma((2, reach, 2)),
            dma((2, reach + 1, 2)), dma((2, reach + 1, 2)),
            dma((peers,)), dma((peers,)),
            dma((n_pair - 1, peers)), dma((n_pair - 1, peers)),
            dma((n_pair - 1,)), dma((n_pair - 1,)),
        ],
        compiler_params=pltpu.CompilerParams(collective_id=0, has_side_effects=True),
    )(meta, own)


def solution(mesh):
    in_specs = (
        P("pair", "split", None),
        P("pair", None, "split"),
        P("pair", None, "split"),
        P(),
        P("pair"),
        P(),
    )
    out_specs = (P("pair", None, None), P("pair", None, None), P("pair", None))
    body = functools.partial(per_device, mesh.shape["pair"], mesh.shape["split"])
    return jax.shard_map(body, mesh=mesh, in_specs=in_specs, out_specs=out_specs, check_vma=False)
```

```python
import functools
import math

import jax
import jax.numpy as jnp
from jax import lax
from jax.experimental import pallas as pl
from jax.experimental.pallas import tpu as pltpu
from jax.sharding import PartitionSpec as P

NT = (((1,), (1,)), ((), ()))
NN = (((1,), (0,)), ((), ()))
PAD = 16
PIECES = 4


def fused(dims, meta, desc_ref, points_ref, normals_ref, pc_ref, ph_ref, pg_ref, own_ref, blocks, src, mine, theirs, feats, tgrams,
          vown, vrecv, ring_send, ring_recv, part_send, part_recv, src_send, src_recv, par_send, par_recv, pose_send, pose_recv):
    n_pair, n_split, hr, width, tasks = dims
    half_ring = n_pair // 2
    reach = half_ring // 2
    n_sub = 2 * n_split
    rows = n_sub * hr
    quarter = hr // 2
    cuts = [0] + [PAD + (q + 1) * quarter for q in range(PIECES)]
    factor = math.log2(math.e) * width ** -0.5
    p = lax.axis_index("pair")
    sp = lax.axis_index("split")
    core = p % 2
    group = p // 2
    partner = p + 1 - 2 * core
    odd = group % 2
    spot = (1 - odd) * (group // 2) + odd * (half_ring - 1 - group // 2)

    def pair_at(where, which):
        where = (where + half_ring) % half_ring
        late = where // reach
        return ((1 - late) * 2 * where + late * (2 * (half_ring - 1 - where) + 1)) * 2 + which

    def remote(a, b, s, r, device):
        return pltpu.make_async_remote_copy(a, b, s, r, device_id=device, device_id_type=pl.DeviceIdType.MESH)

    own_ref[PAD:, :] = desc_ref[0]
    geometry = jnp.concatenate(
        [points_ref[0].astype(jnp.float32), normals_ref[0].astype(jnp.float32), jnp.ones((1, 2 * hr), jnp.float32),
         jnp.zeros((1, 2 * hr), jnp.float32)], axis=0)
    geometry = jnp.concatenate([geometry[:, :hr], geometry[:, hr:]], axis=0).astype(jnp.bfloat16)
    if hr < width:
        own_ref[0:PAD, :] = jnp.zeros((PAD, width), jnp.bfloat16)
    own_ref[0:PAD, :hr] = geometry
    src[sp] = own_ref[...]
    feats[p] = jnp.zeros_like(feats[p])

    barrier = pltpu.get_barrier_semaphore()
    for f in range(1, n_pair):
        pl.semaphore_signal(barrier, inc=1, device_id={"pair": (p + f) % n_pair}, device_id_type=pl.DeviceIdType.MESH)
    for f in range(1, n_split):
        pl.semaphore_signal(barrier, inc=1, device_id={"split": (sp + f) % n_split}, device_id_type=pl.DeviceIdType.MESH)
    pl.semaphore_wait(barrier, n_pair + n_split - 2)

    goal = [pair_at(spot + 1, core), pair_at(spot - 1, core)]

    def slot_of(way, d, which):
        return pair_at(spot - d if way == 0 else spot + d, which)

    def piece(ref, q):
        return ref.at[pl.ds(cuts[q], cuts[q + 1] - cuts[q])]

    def ring_copy(way, d, q):
        slot = slot_of(way, d, core)
        source = own_ref if isinstance(d, int) and d == 0 else blocks.at[slot]
        return remote(piece(source, q), piece(blocks.at[slot], q), ring_send.at[way, d, q], ring_recv.at[way, d, q],
                      {"pair": goal[way]})

    def ring_arrival(way, d, q):
        here = piece(blocks.at[slot_of(way, d, core)], q)
        return remote(here, here, ring_send.at[way, d - 1, q], ring_recv.at[way, d - 1, q], {"pair": goal[way]})

    def part_copy(way, d, q):
        slot = slot_of(way, d, core)
        source = own_ref if isinstance(d, int) and d == 0 else blocks.at[slot]
        return remote(piece(source, q), piece(blocks.at[slot], q), part_send.at[way, d, q], part_recv.at[way, d, q],
                      {"pair": partner})

    def part_arrival(way, d, q):
        here = piece(blocks.at[slot_of(way, d, 1 - core)], q)
        return remote(here, here, part_send.at[way, d, q], part_recv.at[way, d, q], {"pair": partner})

    def src_copy(f, where):
        return remote(own_ref, src.at[where], src_send.at[f - 1], src_recv.at[f - 1], {"split": (sp + f) % n_split})

    def par_copy(index, slot, f):
        return remote(mine.at[slot], theirs.at[f - 1, slot], par_send.at[index, f - 1], par_recv.at[index, f - 1],
                      {"split": (sp + f) % n_split})

    for f in range(1, n_split):
        src_copy(f, sp).start()
    for q in range(PIECES):
        for way in range(2):
            ring_copy(way, 0, q).start()
        part_copy(0, 0, q).start()

    row8 = lax.broadcasted_iota(jnp.int32, (8, hr), 0)

    def attend(slot):
        for u in range(n_sub):
            queries = src[u // 2, pl.ds(PAD + (u % 2) * hr, hr), :]
            scores = [lax.dot_general(blocks[slot, pl.ds(PAD + h * hr, hr), :], queries, NT, preferred_element_type=jnp.float32)
                      for h in range(2)]
            top = jnp.maximum(jnp.max(scores[0], axis=0, keepdims=True), jnp.max(scores[1], axis=0, keepdims=True))
            shape = blocks[slot, 0:PAD, :hr]
            moment = None
            for h in range(2):
                weight = jnp.exp2((scores[h] - top) * factor)
                coarse = weight.astype(jnp.bfloat16)
                fine = (weight - coarse.astype(jnp.float32)).astype(jnp.bfloat16)
                for piece in (coarse, fine):
                    term = lax.dot_general(shape, piece, NN, preferred_element_type=jnp.float32)[8 * h:8 * h + 8]
                    moment = term if moment is None else moment + term
            mine[slot, u] = jnp.where(row8 == 7, top, moment)

    def featurize(index, slot):
        for f in range(1, n_split):
            par_copy(index, slot, f).wait_recv()
        for u in range(n_sub):
            parts = [mine[slot, u]] + [theirs[f, slot, u] for f in range(n_split - 1)]
            top = parts[0][7:8]
            for part in parts[1:]:
                top = jnp.maximum(top, part[7:8])
            total = None
            for part in parts:
                term = part * jnp.exp2((part[7:8] - top) * factor)
                total = term if total is None else total + term
            soft = total / total[6:7]
            y = src[u // 2, 0:PAD, :hr].astype(jnp.float32)[8 * (u % 2):8 * (u % 2) + 8]
            yv = [y[c:c + 1] for c in range(3)]
            mv = [soft[c:c + 1] for c in range(3)]
            nv = [soft[c:c + 1] for c in range(3, 6)]

            def cross(a, b):
                return [a[1] * b[2] - a[2] * b[1], a[2] * b[0] - a[0] * b[2], a[0] * b[1] - a[1] * b[0]]

            residual = nv[0] * (yv[0] - mv[0]) + nv[1] * (yv[1] - mv[1]) + nv[2] * (yv[2] - mv[2])
            zero = jnp.zeros_like(residual)
            minus = [-v for v in cross(mv, nv)] + [-v for v in nv]
            f16 = jnp.concatenate(cross(yv, nv) + nv + [residual, zero] + minus + [residual, zero], axis=0)
            coarse = f16.astype(jnp.bfloat16)
            fine = (f16 - coarse.astype(jnp.float32)).astype(jnp.bfloat16)
            feats[slot, :, u * hr:(u + 1) * hr] = jnp.concatenate([coarse, fine], axis=0)

    def slot_at(index):
        d = (index + 3) // 4
        j = (index + 3) % 4
        way = j % 2
        which = (1 - j // 2) * core + (j // 2) * (1 - core)
        return pair_at(spot - (1 - 2 * way) * d, which)

    def process(index, slot, lagged):
        attend(slot)
        for f in range(1, n_split):
            par_copy(index, slot, f).start()
        if lagged:
            featurize(index - 2, slot_at(index - 2))

    def take_partner(way, d):
        for q in range(PIECES):
            part_arrival(way, d, q).wait_recv()

    def event(d, q, last):
        for way in range(2):
            ring_arrival(way, d, q).wait_recv()
            if last:
                @pl.when(d + 1 < reach)
                def _():
                    ring_copy(way, d, q).start()
                if way == q // 2:
                    @pl.when(d + 1 == reach)
                    def _():
                        ring_copy(way, d, q).start()
            else:
                ring_copy(way, d, q).start()
            part_copy(way, d, q).start()

    for q in range(PIECES):
        event(1, q, reach == 2)
    for f in range(1, n_split):
        src_copy(f, (sp + n_split - f) % n_split).wait_recv()
    take_partner(0, 0)
    process(0, slot_at(0), False)
    process(1, slot_at(1), False)

    def stage(d, carry):
        base = 4 * d - 6
        for q in range(PIECES):
            event(d, q, True)
            if q in (1, 2):
                take_partner(q - 1, d - 1)
            process(base + q, slot_at(base + q), True)
        return carry

    lax.fori_loop(2, reach, stage, 0)
    base = 4 * reach - 6
    final_own = slot_of(0, reach, core)
    final_partner = slot_of(0, reach, 1 - core)
    half_pieces = PIECES // 2
    for k in range(half_pieces):
        for way in range(2):
            q = way * half_pieces + k
            ring_arrival(way, reach, q).wait_recv()
            part_copy(way, reach, q).start()
        if k == 0:
            process(base, slot_at(base), True)
            take_partner(0, reach - 1)
            process(base + 1, slot_at(base + 1), True)
    take_partner(1, reach - 1)
    process(base + 2, slot_at(base + 2), True)
    process(base + 3, final_own, True)
    for way in range(2):
        for k in range(half_pieces):
            part_arrival(way, reach, way * half_pieces + k).wait_recv()
    process(base + 4, final_partner, True)
    featurize(base + 3, final_own)
    featurize(base + 4, final_partner)

    lanes = 8 * n_pair
    row_ids = lax.broadcasted_iota(jnp.int32, (32, rows), 1)
    source_sum = jnp.zeros((8, 16), jnp.float32)
    for k in range(tasks):
        f = feats[meta[k]]
        live = jnp.where(row_ids < meta[tasks + k], f, jnp.zeros_like(f))
        gram = lax.dot_general(live, f, NT, preferred_element_type=jnp.float32)
        gram = gram[:16] + gram[16:]
        gram = (gram[:, :16] + gram[:, 16:]) * (1.0 / rows)
        pc_ref[k] = gram[0:6, 8:14]
        source_sum = source_sum + gram[:8]
        tgrams[k * 8:(k + 1) * 8, :] = gram[8:]
    spread_row = lax.broadcasted_iota(jnp.int32, (16, lanes), 0)
    spread_lane = lax.broadcasted_iota(jnp.int32, (16, lanes), 1)
    highest = lax.Precision.HIGHEST
    spread_target = (spread_lane % 8 == spread_row - 8).astype(jnp.float32)
    spread_source = (spread_lane % 8 == spread_row).astype(jnp.float32)
    wide = lax.dot_general(tgrams[...], spread_target, NN, precision=highest, preferred_element_type=jnp.float32)
    lane_scan = lax.broadcasted_iota(jnp.int32, (8, lanes), 1) // 8
    total = jnp.where(
        lane_scan == p,
        lax.dot_general(source_sum, spread_source, NN, precision=highest, preferred_element_type=jnp.float32), 0.0)
    for k in range(tasks):
        total = total + jnp.where(lane_scan == meta[k], wide[k * 8:(k + 1) * 8], 0.0)
    vown[...] = total
    for f in range(1, n_pair):
        remote(vown, vrecv.at[f - 1], pose_send.at[f - 1], pose_recv.at[f - 1], {"pair": (p + f) % n_pair}).start()
    scan = 0
    for k in range(n_pair):
        scan = scan + k * (meta[2 * tasks + k] == p).astype(jnp.int32)
    for f in range(1, n_pair):
        remote(vown, vrecv.at[f - 1], pose_send.at[f - 1], pose_recv.at[f - 1], {"pair": (p + f) % n_pair}).wait_recv()
    for f in range(n_pair - 1):
        total = total + vrecv[f]
    total = jnp.where(lane_scan == scan, total, 0.0) * (1.0 / tasks)
    gather_row = lax.broadcasted_iota(jnp.int32, (8, lanes), 0)
    gather_lane = lax.broadcasted_iota(jnp.int32, (8, lanes), 1)
    pick = (gather_lane % 8 == gather_row).astype(jnp.float32)
    result = lax.dot_general(total, pick, NT, precision=highest, preferred_element_type=jnp.float32)
    ph_ref[0] = result[0:6, 0:6]
    pg_ref[...] = result[6:7, 0:6]
    for f in range(1, n_pair):
        remote(vown, vrecv.at[f - 1], pose_send.at[f - 1], pose_recv.at[f - 1], {"pair": (p + f) % n_pair}).wait_send()
    for f in range(1, n_split):
        src_copy(f, sp).wait_send()

        def sent(index, carry):
            par_copy(index, slot_at(index), f).wait_send()
            return carry

        lax.fori_loop(0, n_pair - 2, sent, 0)
        par_copy(n_pair - 2, final_partner, f).wait_send()
    for q in range(PIECES):
        part_copy(0, 0, q).wait_send()
        for way in range(2):
            ring_copy(way, 0, q).wait_send()
            if way == q // half_pieces:
                ring_copy(way, reach - 1, q).wait_send()
                part_copy(way, reach, q).wait_send()

    def drained(d, carry):
        for q in range(PIECES):
            for way in range(2):
                part_copy(way, d, q).wait_send()

                @pl.when(d + 1 < reach)
                def _():
                    ring_copy(way, d, q).wait_send()
        return carry

    lax.fori_loop(1, reach, drained, 0)


def per_device(n_pair, n_split, descriptors, points, normals, pair_list, intersection, pose_index):
    block_rows, width = descriptors.shape[1:]
    hr = block_rows // 2
    tasks = intersection.shape[0]
    p = lax.axis_index("pair")
    targets = lax.dynamic_slice_in_dim(pair_list[:, 1], p * tasks, tasks, 0)
    meta = jnp.concatenate([targets, intersection, pose_index])
    n_sub = 2 * n_split
    reach = n_pair // 4
    peers = max(n_split - 1, 1)
    dims = (n_pair, n_split, hr, width, tasks)
    dma = pltpu.SemaphoreType.DMA
    vmem = pl.BlockSpec(memory_space=pltpu.VMEM)
    return pl.pallas_call(
        functools.partial(fused, dims),
        out_shape=(
            jax.ShapeDtypeStruct((tasks, 6, 6), jnp.float32),
            jax.ShapeDtypeStruct((1, 6, 6), jnp.float32),
            jax.ShapeDtypeStruct((1, 6), jnp.float32),
        ),
        in_specs=[pl.BlockSpec(memory_space=pltpu.SMEM), vmem, vmem, vmem],
        out_specs=(vmem, vmem, vmem),
        scratch_shapes=[
            pltpu.VMEM((block_rows + PAD, width), jnp.bfloat16),
            pltpu.VMEM((n_pair, block_rows + PAD, width), jnp.bfloat16),
            pltpu.VMEM((n_split, block_rows + PAD, width), jnp.bfloat16),
            pltpu.VMEM((n_pair, n_sub, 8, hr), jnp.float32),
            pltpu.VMEM((peers, n_pair, n_sub, 8, hr), jnp.float32),
            pltpu.VMEM((n_pair, 32, n_sub * hr), jnp.bfloat16),
            pltpu.VMEM((tasks * 8, 16), jnp.float32),
            pltpu.VMEM((8, 8 * n_pair), jnp.float32),
            pltpu.VMEM((n_pair - 1, 8, 8 * n_pair), jnp.float32),
            dma((2, reach, PIECES)), dma((2, reach, PIECES)),
            dma((2, reach + 1, PIECES)), dma((2, reach + 1, PIECES)),
            dma((peers,)), dma((peers,)),
            dma((n_pair - 1, peers)), dma((n_pair - 1, peers)),
            dma((n_pair - 1,)), dma((n_pair - 1,)),
        ],
        compiler_params=pltpu.CompilerParams(collective_id=0, has_side_effects=True),
    )(meta, descriptors, points, normals)


def solution(mesh):
    in_specs = (
        P("pair", "split", None),
        P("pair", None, "split"),
        P("pair", None, "split"),
        P(),
        P("pair"),
        P(),
    )
    out_specs = (P("pair", None, None), P("pair", None, None), P("pair", None))
    body = functools.partial(per_device, mesh.shape["pair"], mesh.shape["split"])
    return jax.shard_map(body, mesh=mesh, in_specs=in_specs, out_specs=out_specs, check_vma=False)
```

```python
import functools
import math

import jax
import jax.numpy as jnp
from jax import lax
from jax.experimental import pallas as pl
from jax.experimental.pallas import tpu as pltpu
from jax.sharding import PartitionSpec as P

NT = (((1,), (1,)), ((), ()))
NN = (((1,), (0,)), ((), ()))
PAD = 16
PIECES = 4


def fused(dims, meta, desc_ref, points_ref, normals_ref, pc_ref, ph_ref, pg_ref, own_ref, blocks, src, mine, theirs, feats, tgrams,
          vown, vrecv, ring_send, ring_recv, part_send, part_recv, src_send, src_recv, par_send, par_recv, pose_send, pose_recv):
    n_pair, n_split, hr, width, tasks = dims
    half_ring = n_pair // 2
    reach = half_ring // 2
    n_sub = 2 * n_split
    rows = n_sub * hr
    quarter = hr // 2
    cuts = [0] + [2 * PAD + (q + 1) * quarter for q in range(PIECES)]
    factor = math.log2(math.e) * width ** -0.5
    p = lax.axis_index("pair")
    sp = lax.axis_index("split")
    core = p % 2
    group = p // 2
    partner = p + 1 - 2 * core
    odd = group % 2
    spot = (1 - odd) * (group // 2) + odd * (half_ring - 1 - group // 2)

    def pair_at(where, which):
        where = (where + half_ring) % half_ring
        late = where // reach
        return ((1 - late) * 2 * where + late * (2 * (half_ring - 1 - where) + 1)) * 2 + which

    def remote(a, b, s, r, device):
        return pltpu.make_async_remote_copy(a, b, s, r, device_id=device, device_id_type=pl.DeviceIdType.MESH)

    own_ref[2 * PAD:, :] = desc_ref[0]
    geometry = jnp.concatenate(
        [points_ref[0].astype(jnp.float32), normals_ref[0].astype(jnp.float32), jnp.ones((1, 2 * hr), jnp.float32),
         jnp.zeros((PAD - 7, 2 * hr), jnp.float32)], axis=0)
    geometry = jnp.concatenate([geometry[:, :hr], geometry[:, hr:]], axis=0).astype(jnp.bfloat16)
    if hr < width:
        own_ref[0:2 * PAD, :] = jnp.zeros((2 * PAD, width), jnp.bfloat16)
    own_ref[0:2 * PAD, :hr] = geometry
    src[sp] = own_ref[...]
    feats[p] = jnp.zeros_like(feats[p])

    barrier = pltpu.get_barrier_semaphore()
    for f in range(1, n_pair):
        pl.semaphore_signal(barrier, inc=1, device_id={"pair": (p + f) % n_pair}, device_id_type=pl.DeviceIdType.MESH)
    for f in range(1, n_split):
        pl.semaphore_signal(barrier, inc=1, device_id={"split": (sp + f) % n_split}, device_id_type=pl.DeviceIdType.MESH)
    pl.semaphore_wait(barrier, n_pair + n_split - 2)

    goal = [pair_at(spot + 1, core), pair_at(spot - 1, core)]

    def slot_of(way, d, which):
        return pair_at(spot - d if way == 0 else spot + d, which)

    def piece(ref, q):
        return ref.at[pl.ds(cuts[q], cuts[q + 1] - cuts[q])]

    def ring_copy(way, d, q):
        slot = slot_of(way, d, core)
        source = own_ref if isinstance(d, int) and d == 0 else blocks.at[slot]
        return remote(piece(source, q), piece(blocks.at[slot], q), ring_send.at[way, d, q], ring_recv.at[way, d, q],
                      {"pair": goal[way]})

    def ring_arrival(way, d, q):
        here = piece(blocks.at[slot_of(way, d, core)], q)
        return remote(here, here, ring_send.at[way, d - 1, q], ring_recv.at[way, d - 1, q], {"pair": goal[way]})

    def part_copy(way, d, q):
        slot = slot_of(way, d, core)
        source = own_ref if isinstance(d, int) and d == 0 else blocks.at[slot]
        return remote(piece(source, q), piece(blocks.at[slot], q), part_send.at[way, d, q], part_recv.at[way, d, q],
                      {"pair": partner})

    def part_arrival(way, d, q):
        here = piece(blocks.at[slot_of(way, d, 1 - core)], q)
        return remote(here, here, part_send.at[way, d, q], part_recv.at[way, d, q], {"pair": partner})

    def src_copy(f, where):
        return remote(own_ref, src.at[where], src_send.at[f - 1], src_recv.at[f - 1], {"split": (sp + f) % n_split})

    def par_copy(index, slot, f):
        return remote(mine.at[slot], theirs.at[f - 1, slot], par_send.at[index, f - 1], par_recv.at[index, f - 1],
                      {"split": (sp + f) % n_split})

    for f in range(1, n_split):
        src_copy(f, sp).start()
    for q in range(PIECES):
        for way in range(2):
            ring_copy(way, 0, q).start()
        part_copy(0, 0, q).start()

    row8 = lax.broadcasted_iota(jnp.int32, (8, hr), 0)

    def attend(slot):
        for u in range(n_sub):
            queries = src[u // 2, pl.ds(2 * PAD + (u % 2) * hr, hr), :]
            scores = [lax.dot_general(blocks[slot, pl.ds(2 * PAD + h * hr, hr), :], queries, NT, preferred_element_type=jnp.float32)
                      for h in range(2)]
            top = jnp.maximum(jnp.max(scores[0], axis=0, keepdims=True), jnp.max(scores[1], axis=0, keepdims=True))
            moment = None
            for h in range(2):
                shape = blocks[slot, h * PAD:(h + 1) * PAD, :hr]
                weight = jnp.exp2((scores[h] - top) * factor)
                coarse = weight.astype(jnp.bfloat16)
                fine = (weight - coarse.astype(jnp.float32)).astype(jnp.bfloat16)
                for piece in (coarse, fine):
                    term = lax.dot_general(shape, piece, NN, preferred_element_type=jnp.float32)
                    moment = term if moment is None else moment + term
            mine[slot, u] = jnp.where(row8 == 7, top, moment[:8])

    def featurize(index, slot):
        for f in range(1, n_split):
            par_copy(index, slot, f).wait_recv()
        for u in range(n_sub):
            parts = [mine[slot, u]] + [theirs[f, slot, u] for f in range(n_split - 1)]
            top = parts[0][7:8]
            for part in parts[1:]:
                top = jnp.maximum(top, part[7:8])
            total = None
            for part in parts:
                term = part * jnp.exp2((part[7:8] - top) * factor)
                total = term if total is None else total + term
            soft = total / total[6:7]
            y = src[u // 2, (u % 2) * PAD:(u % 2) * PAD + PAD, :hr].astype(jnp.float32)
            yv = [y[c:c + 1] for c in range(3)]
            mv = [soft[c:c + 1] for c in range(3)]
            nv = [soft[c:c + 1] for c in range(3, 6)]

            def cross(a, b):
                return [a[1] * b[2] - a[2] * b[1], a[2] * b[0] - a[0] * b[2], a[0] * b[1] - a[1] * b[0]]

            residual = nv[0] * (yv[0] - mv[0]) + nv[1] * (yv[1] - mv[1]) + nv[2] * (yv[2] - mv[2])
            zero = jnp.zeros_like(residual)
            minus = [-v for v in cross(mv, nv)] + [-v for v in nv]
            f16 = jnp.concatenate(cross(yv, nv) + nv + [residual, zero] + minus + [residual, zero], axis=0)
            coarse = f16.astype(jnp.bfloat16)
            fine = (f16 - coarse.astype(jnp.float32)).astype(jnp.bfloat16)
            feats[slot, :, u * hr:(u + 1) * hr] = jnp.concatenate([coarse, fine], axis=0)

    def slot_at(index):
        d = (index + 3) // 4
        j = (index + 3) % 4
        way = j % 2
        which = (1 - j // 2) * core + (j // 2) * (1 - core)
        return pair_at(spot - (1 - 2 * way) * d, which)

    def process(index, slot, lagged):
        attend(slot)
        for f in range(1, n_split):
            par_copy(index, slot, f).start()

    def take_partner(way, d):
        for q in range(PIECES):
            part_arrival(way, d, q).wait_recv()

    def event(d, q, last):
        for way in range(2):
            ring_arrival(way, d, q).wait_recv()
            if last:
                @pl.when(d + 1 < reach)
                def _():
                    ring_copy(way, d, q).start()
                if way == q // 2:
                    @pl.when(d + 1 == reach)
                    def _():
                        ring_copy(way, d, q).start()
            else:
                ring_copy(way, d, q).start()
            part_copy(way, d, q).start()

    for q in range(PIECES):
        event(1, q, reach == 2)
    for f in range(1, n_split):
        src_copy(f, (sp + n_split - f) % n_split).wait_recv()
    take_partner(0, 0)
    process(0, slot_at(0), False)
    process(1, slot_at(1), False)

    def stage(d, carry):
        base = 4 * d - 6
        for q in range(PIECES):
            event(d, q, True)
            if q in (1, 2):
                take_partner(q - 1, d - 1)
            process(base + q, slot_at(base + q), True)
        return carry

    lax.fori_loop(2, reach, stage, 0)
    base = 4 * reach - 6
    final_own = slot_of(0, reach, core)
    final_partner = slot_of(0, reach, 1 - core)
    half_pieces = PIECES // 2
    for k in range(half_pieces):
        for way in range(2):
            q = way * half_pieces + k
            ring_arrival(way, reach, q).wait_recv()
            part_copy(way, reach, q).start()
        if k == 0:
            process(base, slot_at(base), True)
            take_partner(0, reach - 1)
            process(base + 1, slot_at(base + 1), True)
    take_partner(1, reach - 1)
    process(base + 2, slot_at(base + 2), True)
    process(base + 3, final_own, True)
    for way in range(2):
        for k in range(half_pieces):
            part_arrival(way, reach, way * half_pieces + k).wait_recv()
    process(base + 4, final_partner, True)
    def features(index, carry):
        featurize(index, slot_at(index))
        return carry

    lax.fori_loop(0, n_pair - 2, features, 0)
    featurize(base + 4, final_partner)

    lanes = 8 * n_pair
    row_ids = lax.broadcasted_iota(jnp.int32, (32, rows), 1)
    source_sum = jnp.zeros((8, 16), jnp.float32)
    for k in range(tasks):
        f = feats[meta[k]]
        live = jnp.where(row_ids < meta[tasks + k], f, jnp.zeros_like(f))
        gram = lax.dot_general(live, f, NT, preferred_element_type=jnp.float32)
        gram = gram[:16] + gram[16:]
        gram = (gram[:, :16] + gram[:, 16:]) * (1.0 / rows)
        pc_ref[k] = gram[0:6, 8:14]
        source_sum = source_sum + gram[:8]
        tgrams[k * 8:(k + 1) * 8, :] = gram[8:]
    spread_row = lax.broadcasted_iota(jnp.int32, (16, lanes), 0)
    spread_lane = lax.broadcasted_iota(jnp.int32, (16, lanes), 1)
    highest = lax.Precision.HIGHEST
    spread_target = (spread_lane % 8 == spread_row - 8).astype(jnp.float32)
    spread_source = (spread_lane % 8 == spread_row).astype(jnp.float32)
    wide = lax.dot_general(tgrams[...], spread_target, NN, precision=highest, preferred_element_type=jnp.float32)
    lane_scan = lax.broadcasted_iota(jnp.int32, (8, lanes), 1) // 8
    total = jnp.where(
        lane_scan == p,
        lax.dot_general(source_sum, spread_source, NN, precision=highest, preferred_element_type=jnp.float32), 0.0)
    for k in range(tasks):
        total = total + jnp.where(lane_scan == meta[k], wide[k * 8:(k + 1) * 8], 0.0)
    vown[...] = total
    for f in range(1, n_pair):
        remote(vown, vrecv.at[f - 1], pose_send.at[f - 1], pose_recv.at[f - 1], {"pair": (p + f) % n_pair}).start()
    scan = 0
    for k in range(n_pair):
        scan = scan + k * (meta[2 * tasks + k] == p).astype(jnp.int32)
    for f in range(1, n_pair):
        remote(vown, vrecv.at[f - 1], pose_send.at[f - 1], pose_recv.at[f - 1], {"pair": (p + f) % n_pair}).wait_recv()
    for f in range(n_pair - 1):
        total = total + vrecv[f]
    total = jnp.where(lane_scan == scan, total, 0.0) * (1.0 / tasks)
    gather_row = lax.broadcasted_iota(jnp.int32, (8, lanes), 0)
    gather_lane = lax.broadcasted_iota(jnp.int32, (8, lanes), 1)
    pick = (gather_lane % 8 == gather_row).astype(jnp.float32)
    result = lax.dot_general(total, pick, NT, precision=highest, preferred_element_type=jnp.float32)
    ph_ref[0] = result[0:6, 0:6]
    pg_ref[...] = result[6:7, 0:6]
    for f in range(1, n_pair):
        remote(vown, vrecv.at[f - 1], pose_send.at[f - 1], pose_recv.at[f - 1], {"pair": (p + f) % n_pair}).wait_send()
    for f in range(1, n_split):
        src_copy(f, sp).wait_send()

        def sent(index, carry):
            par_copy(index, slot_at(index), f).wait_send()
            return carry

        lax.fori_loop(0, n_pair - 2, sent, 0)
        par_copy(n_pair - 2, final_partner, f).wait_send()
    for q in range(PIECES):
        part_copy(0, 0, q).wait_send()
        for way in range(2):
            ring_copy(way, 0, q).wait_send()
            if way == q // half_pieces:
                ring_copy(way, reach - 1, q).wait_send()
                part_copy(way, reach, q).wait_send()

    def drained(d, carry):
        for q in range(PIECES):
            for way in range(2):
                part_copy(way, d, q).wait_send()

                @pl.when(d + 1 < reach)
                def _():
                    ring_copy(way, d, q).wait_send()
        return carry

    lax.fori_loop(1, reach, drained, 0)


def per_device(n_pair, n_split, descriptors, points, normals, pair_list, intersection, pose_index):
    block_rows, width = descriptors.shape[1:]
    hr = block_rows // 2
    tasks = intersection.shape[0]
    p = lax.axis_index("pair")
    targets = lax.dynamic_slice_in_dim(pair_list[:, 1], p * tasks, tasks, 0)
    meta = jnp.concatenate([targets, intersection, pose_index])
    n_sub = 2 * n_split
    reach = n_pair // 4
    peers = max(n_split - 1, 1)
    dims = (n_pair, n_split, hr, width, tasks)
    dma = pltpu.SemaphoreType.DMA
    vmem = pl.BlockSpec(memory_space=pltpu.VMEM)
    return pl.pallas_call(
        functools.partial(fused, dims),
        out_shape=(
            jax.ShapeDtypeStruct((tasks, 6, 6), jnp.float32),
            jax.ShapeDtypeStruct((1, 6, 6), jnp.float32),
            jax.ShapeDtypeStruct((1, 6), jnp.float32),
        ),
        in_specs=[pl.BlockSpec(memory_space=pltpu.SMEM), vmem, vmem, vmem],
        out_specs=(vmem, vmem, vmem),
        scratch_shapes=[
            pltpu.VMEM((block_rows + 2 * PAD, width), jnp.bfloat16),
            pltpu.VMEM((n_pair, block_rows + 2 * PAD, width), jnp.bfloat16),
            pltpu.VMEM((n_split, block_rows + 2 * PAD, width), jnp.bfloat16),
            pltpu.VMEM((n_pair, n_sub, 8, hr), jnp.float32),
            pltpu.VMEM((peers, n_pair, n_sub, 8, hr), jnp.float32),
            pltpu.VMEM((n_pair, 32, n_sub * hr), jnp.bfloat16),
            pltpu.VMEM((tasks * 8, 16), jnp.float32),
            pltpu.VMEM((8, 8 * n_pair), jnp.float32),
            pltpu.VMEM((n_pair - 1, 8, 8 * n_pair), jnp.float32),
            dma((2, reach, PIECES)), dma((2, reach, PIECES)),
            dma((2, reach + 1, PIECES)), dma((2, reach + 1, PIECES)),
            dma((peers,)), dma((peers,)),
            dma((n_pair - 1, peers)), dma((n_pair - 1, peers)),
            dma((n_pair - 1,)), dma((n_pair - 1,)),
        ],
        compiler_params=pltpu.CompilerParams(collective_id=0, has_side_effects=True),
    )(meta, descriptors, points, normals)


def solution(mesh):
    in_specs = (
        P("pair", "split", None),
        P("pair", None, "split"),
        P("pair", None, "split"),
        P(),
        P("pair"),
        P(),
    )
    out_specs = (P("pair", None, None), P("pair", None, None), P("pair", None))
    body = functools.partial(per_device, mesh.shape["pair"], mesh.shape["split"])
    return jax.shard_map(body, mesh=mesh, in_specs=in_specs, out_specs=out_specs, check_vma=False)
```
